32 devices in a mesh: run: 8 (over z, core), mz: 4 (over y, x).
Axes of the slice: x: 2, y: 2, z: 4, core: 2. Of those that a mesh axis runs over, the one named last changes fastest.
Arguments:
- lcms: bfloat16 [512, 256, 4096], P('run', None, 'mz'), may hold values from -600 to 600
- spectra: float32 [512, 65536], P('run', 'mz'), may hold values from -200 to 200
- scan_factor: float32 [64, 256], replicated, may hold values from 0.05 to 0.9
- mz_factor: float32 [64, 4096], P(None, 'mz'), may hold values from 0 to 1.7
- ppm_factor: float32 [64, 65536], P(None, 'mz'), may hold values from 0 to 1.7
Outputs:
- sample_factor: float32 [512, 64], P('run')
- ppm_new: float32 [64, 65536], P(None, ('mz', 'run'))
The draws below stay inside these ranges and needn't reach their ends.
All inputs are finite; a program needn't handle non-finite values.
Results may differ from the reference program's by a relative error of at most 0.0048.
Values sent between devices are 32-bit elements; how exact they have to be, the bound alone decides.
No kernel may reach another device: no remote copies, remote signals or barrier semaphores. Data moves between devices by JAX's collectives and lax.ppermute only.
A program may use at most 128 MiB of HBM per device.

```python
import jax
import jax.numpy as jnp
from jax import lax

RUN_DEV = 64
SCANS = 256
MZ = 4096
PPM = 65536
RANK = 64
RUNS = 512


def ramped_factor(key, columns):
    first_key = jax.random.fold_in(key, 0)
    ramp = 0.6 + 1.2 * jnp.arange(columns, dtype=jnp.float32) / (columns - 1)
    values = jax.random.uniform(first_key, (RANK, columns), jnp.float32, 0.05, 0.9)
    return values * ramp[None, :]


def draw_mz_factor(key, part):
    return ramped_factor(jax.random.fold_in(key, 11), MZ)


def draw_ppm_factor(key, part):
    return ramped_factor(jax.random.fold_in(key, 23), PPM)


def shard_levels(rng, shape, cuts, least, largest):
    level, own = 1.0, jax.random.fold_in(rng, 6)
    for dim, blocks in cuts:
        heights = jnp.exp(jax.random.uniform(jax.random.fold_in(own, dim), (blocks,), jnp.float32, least / len(cuts), largest / len(cuts)))
        level = level * jnp.repeat(heights, shape[dim] // blocks).reshape([-1 if axis == dim else 1 for axis in range(len(shape))])
    return level


def centred(own_key, shape, deviation, bound, shards=(), kind=jnp.bfloat16):
    values = jax.random.normal(own_key, shape, jnp.float32) * deviation
    if len(shards) > 0:
        values = shard_levels(own_key, shape, shards, -0.22, 0.18) * values
    return jnp.clip(values, min=-bound, max=bound).astype(kind)


def setup_inputs(seed: int = 0) -> dict:
    arg_keys = jax.random.split(jax.random.key(seed), 6)
    lcms = centred(arg_keys[0], (RUNS, SCANS, MZ), 100.0, 600.0, ((0, 8), (2, 4)))
    spectra = centred(arg_keys[1], (RUNS, PPM), 32.0, 200.0, ((0, 8), (1, 4)), jnp.float32)
    scan_factor = jnp.clip(jax.random.uniform(arg_keys[2], (RANK, SCANS), jnp.float32, 0.05, 0.9), 0.05, 0.9)
    mz_factor = draw_mz_factor(jax.random.fold_in(arg_keys[5], 71), 0)
    ppm_factor = draw_ppm_factor(jax.random.fold_in(arg_keys[5], 71), 0)
    return {"lcms": lcms, "spectra": spectra, "scan_factor": scan_factor, "mz_factor": mz_factor, "ppm_factor": ppm_factor}


def solve_rows(gram_matrix, right_rows):
    lower_factor = jnp.linalg.cholesky(gram_matrix)
    return jax.scipy.linalg.cho_solve((lower_factor, True), right_rows.T).T

def reference(lcms, spectra, scan_factor, mz_factor, ppm_factor):
    highest = lax.Precision.HIGHEST
    scan_bf = scan_factor.astype(jnp.bfloat16).astype(jnp.float32)
    blocks = lcms.reshape(RUNS // RUN_DEV, RUN_DEV, SCANS, MZ)

    def one_block(run_block):
        tensor = jnp.einsum('ijk,rj->irk', run_block.astype(jnp.float32), scan_bf, precision=highest)
        return jnp.sum(tensor * mz_factor[None], axis=2)
    lcms_part = lax.map(one_block, blocks).reshape(RUNS, RANK)
    scan_gram = jnp.dot(scan_factor, scan_factor.T, precision=highest)
    mz_gram = jnp.dot(mz_factor, mz_factor.T, precision=highest)
    ppm_gram = jnp.dot(ppm_factor, ppm_factor.T, precision=highest)
    lcms_gram = scan_gram * mz_gram
    nmr_part = lax.dot_general(spectra, ppm_factor, (((1,), (1,)), ((), ())), precision=highest)
    sample_first = solve_rows(lcms_gram + ppm_gram, lcms_part + nmr_part)
    sample_gram = jnp.dot(sample_first.T, sample_first, precision=highest)
    projected = jnp.dot(sample_first.T, spectra, precision=highest)
    ppm_new = jax.scipy.linalg.cho_solve((jnp.linalg.cholesky(sample_gram), True), projected)
    nmr_fit = lax.dot_general(spectra, ppm_new, (((1,), (1,)), ((), ())), precision=highest)
    new_gram = jnp.dot(ppm_new, ppm_new.T, precision=highest)
    sample_factor = solve_rows(lcms_gram + new_gram, lcms_part + nmr_fit)
    return (sample_factor, ppm_new)
```

```python
import functools

import jax
import jax.numpy as jnp
from jax import lax
from jax.experimental import pallas as pl
from jax.experimental.pallas import tpu as pltpu
from jax.sharding import PartitionSpec as P


F32, BF16 = jnp.float32, jnp.bfloat16
HIGHEST = lax.Precision.HIGHEST
NT = (((1,), (1,)), ((), ()))


def split(values):
    high = values.astype(BF16)
    return high, (values - high.astype(F32)).astype(BF16)


def stack_split(blocks):
    pairs = [split(block) for block in blocks]
    return jnp.concatenate([pair[0] for pair in pairs] + [pair[1] for pair in pairs], axis=0)


def cost(flops, transferred):
    return pl.CostEstimate(flops=int(flops), bytes_accessed=int(transferred), transcendentals=0)


def whole(shape):
    return pl.BlockSpec(shape, lambda *_: (0,) * len(shape))


def nmr_body(blocks, core_ref, *refs):
    spectra_refs, ppm_refs = refs[: 2 * blocks], refs[2 * blocks : 4 * blocks]
    mz_ref, part_ref, keep_ref, send_ref, total = refs[4 * blocks :]
    piece = pl.program_id(0)
    rank = mz_ref.shape[0]

    @pl.when(piece == 0)
    def _():
        total[...] = jnp.zeros_like(total)
        channels = stack_split([mz_ref[...]])
        products = lax.dot_general(channels, channels, NT, preferred_element_type=F32)
        rows = products[:rank] + products[rank:]
        gram = rows[:, :rank] + rows[:, rank:]
        part_ref[rank:, :] = jnp.concatenate([gram, gram], axis=1)

    for core in (0, 1):
        even = jnp.concatenate([spectra_refs[2 * b + core][...] for b in range(blocks)], axis=1)
        positions = stack_split(
            [jnp.concatenate([ppm_refs[2 * b + core][...] for b in range(blocks)], axis=1)]
        )
        left = jnp.concatenate([stack_split([even]), positions], axis=0)
        total[...] += lax.dot_general(left, positions, NT, preferred_element_type=F32)

        @pl.when(core_ref[0] == core)
        def _():
            keep_ref[0] = even

        @pl.when(core_ref[0] != core)
        def _():
            send_ref[0] = even

    @pl.when(piece == pl.num_programs(0) - 1)
    def _():
        samples = spectra_refs[0].shape[0]
        products = total[...]
        fit = products[:samples] + products[samples : 2 * samples]
        gram = products[2 * samples : 2 * samples + rank] + products[2 * samples + rank :]
        part_ref[:rank, :] = jnp.concatenate(
            [fit[:, :rank] + fit[:, rank:], gram[:, :rank] + gram[:, rank:]], axis=1
        )


def nmr_pass(core, spectra, ppm_factor, mz_factor, blocks, pieces):
    samples, positions = spectra.shape
    rank, channels = mz_factor.shape
    width = positions // (2 * blocks * pieces)

    def columns(rows):
        return [
            pl.BlockSpec((rows, width), functools.partial(lambda b, k, c: (0, b * pieces + k), b))
            for b in range(2 * blocks)
        ]

    sorted_shape = jax.ShapeDtypeStruct((pieces, samples, blocks * width), F32)
    return pl.pallas_call(
        functools.partial(nmr_body, blocks),
        name="nmr_pass",
        grid_spec=pltpu.PrefetchScalarGridSpec(
            num_scalar_prefetch=1,
            grid=(pieces,),
            in_specs=columns(samples) + columns(rank) + [whole((rank, channels))],
            out_specs=[whole((2 * rank, 2 * rank))]
            + [pl.BlockSpec((1, samples, blocks * width), lambda k, c: (k, 0, 0))] * 2,
            scratch_shapes=[pltpu.VMEM((2 * samples + 2 * rank, 2 * rank), F32)],
        ),
        out_shape=[jax.ShapeDtypeStruct((2 * rank, 2 * rank), F32), sorted_shape, sorted_shape],
        cost_estimate=cost(2 * 256 * 256 * positions, 4 * 3 * 64 * positions),
    )(core, *([spectra] * (2 * blocks)), *([ppm_factor] * (2 * blocks)), mz_factor)


def lcms_body(lcms_ref, scan_ref, mz_ref, out_ref, weights, scans):
    rank = mz_ref.shape[0]

    @pl.when(pl.program_id(0) == 0)
    def _():
        channels = mz_ref[...].T
        high, low = split(channels)
        weights[...] = jnp.concatenate([high, low], axis=1)
        scan = scan_ref[...].astype(BF16).astype(F32).T
        scans[...] = jnp.concatenate([scan, scan], axis=1)

    count, steps, channels = lcms_ref.shape
    inner = jnp.dot(
        lcms_ref[...].reshape(count * steps, channels), weights[...], preferred_element_type=F32
    )
    sums = jnp.sum(inner.reshape(count, steps, 2 * rank) * scans[...][None], axis=1)
    out_ref[...] = sums + pltpu.roll(sums, rank, 1)


def lcms_pass(lcms, scan_factor, mz_factor):
    samples, steps, channels = lcms.shape
    rank = mz_factor.shape[0]
    count = 8
    return pl.pallas_call(
        lcms_body,
        name="lcms_pass",
        grid=(samples // count,),
        in_specs=[
            pl.BlockSpec((count, steps, channels), lambda i: (i, 0, 0)),
            whole(scan_factor.shape),
            whole(mz_factor.shape),
        ],
        out_specs=pl.BlockSpec((count, 2 * rank), lambda i: (i, 0)),
        out_shape=jax.ShapeDtypeStruct((samples, 2 * rank), F32),
        scratch_shapes=[
            pltpu.VMEM((channels, 2 * rank), BF16),
            pltpu.VMEM((steps, 2 * rank), F32),
        ],
        cost_estimate=cost(2 * samples * steps * channels * 256, 2 * samples * steps * channels),
    )(lcms, scan_factor, mz_factor)


def weights_body(own_ref, other_ref, left_ref, gram_ref):
    rank = own_ref.shape[1]
    own_high, own_low = split(own_ref[...].T)
    other_high, other_low = split(other_ref[...].T)
    left = jnp.concatenate(
        [
            jnp.concatenate([own_high, other_high, own_high, other_high], axis=1),
            jnp.concatenate([own_low, other_low, own_low, other_low], axis=1),
        ],
        axis=0,
    )
    left_ref[...] = left
    right = stack_split([own_ref[...], other_ref[...]])
    products = jnp.dot(left, right, preferred_element_type=F32)
    gram = products[:rank] + products[rank:]
    gram_ref[...] = jnp.concatenate([gram, gram], axis=1)


def weights_pass(own, other):
    samples, rank = own.shape
    return pl.pallas_call(
        weights_body,
        name="weights_pass",
        out_shape=[
            jax.ShapeDtypeStruct((2 * rank, 4 * samples), BF16),
            jax.ShapeDtypeStruct((rank, 2 * rank), F32),
        ],
        cost_estimate=cost(2 * 128 * 256 * 64, 131072),
    )(own, other)


def project_body(left_ref, own_ref, other_ref, *refs):
    rank, columns = left_ref.shape[0] // 2, own_ref.shape[2]
    outs = [ref for ref in refs if ref.shape[1] >= columns]
    extras = [ref for ref in refs if ref.shape[1] < columns]
    right = stack_split([own_ref[0], other_ref[0]])
    products = jnp.dot(left_ref[...], right, preferred_element_type=F32)
    values = products[:rank] + products[rank:]
    for k, out_ref in enumerate(outs):

        @pl.when(pl.program_id(0) == k)
        def _():
            out_ref[:, :columns] = values

    for extra in extras:
        outs[0][:, columns:] = extra[...]


def project_pass(left, own, other, extra, first, count):
    _, samples, columns = own.shape
    rank = left.shape[0] // 2
    extras = [] if extra is None else [extra]
    wide = columns + sum(e.shape[1] for e in extras)
    piece = pl.BlockSpec((1, samples, columns), lambda k: (first + k, 0, 0))
    return pl.pallas_call(
        project_body,
        grid=(count,),
        in_specs=[whole(left.shape), piece, piece] + [whole(e.shape) for e in extras],
        out_specs=[whole((rank, wide))] * count,
        out_shape=[pltpu.VMEM((rank, wide), F32)] * count,
        cost_estimate=cost(2 * 256 * 256 * columns * count, 12 * 64 * columns * count),
    )(left, own, other, *extras)


def fit_body(count, *refs):
    sweeps, refs = refs[: 4 * count], refs[4 * count :]
    own_sum, other_sum, own_ref, other_ref, own_out, other_out = refs[:6]
    _, samples, _ = own_ref.shape
    rank = own_sum.shape[1] // 2
    sums = None
    for k in range(count):
        part, inward, across, outward = (ref[...] for ref in sweeps[4 * k : 4 * k + 4])
        total = part + inward + across + outward
        refs[6 + k][...] = total
        right = stack_split([total])
        rows = jnp.concatenate([stack_split([own_ref[k], other_ref[k]]), right], axis=0)
        products = lax.dot_general(rows, right, NT, preferred_element_type=F32)
        sums = products if sums is None else sums + products
    sums = sums[:, :rank] + sums[:, rank:]
    own_fit = sums[:samples] + sums[2 * samples : 3 * samples]
    other_fit = sums[samples : 2 * samples] + sums[3 * samples : 4 * samples]
    gram = sums[4 * samples : 4 * samples + rank] + sums[4 * samples + rank :]
    own_out[...] = own_sum[...] + jnp.concatenate([own_fit, gram], axis=1)
    other_out[...] = other_sum[...] + jnp.concatenate([other_fit, gram], axis=1)


def fit_pass(sweeps, own_sum, other_sum, own, other, first):
    _, samples, columns = own.shape
    count, rank = len(sweeps), own_sum.shape[1] // 2
    shape = jax.ShapeDtypeStruct((samples, 2 * rank), F32)
    pieces = pl.BlockSpec((count, samples, columns), lambda i: (first // count, 0, 0))
    arrays = [array for sweep in sweeps for array in sweep]
    own_sum, other_sum, *totals = pl.pallas_call(
        functools.partial(fit_body, count),
        grid=(1,),
        in_specs=[whole((rank, columns))] * len(arrays)
        + [whole(own_sum.shape), whole(other_sum.shape), pieces, pieces],
        out_specs=[whole(shape.shape)] * 2 + [whole((rank, columns))] * count,
        out_shape=[shape, shape] + [jax.ShapeDtypeStruct((rank, columns), F32)] * count,
        cost_estimate=cost(2 * 384 * 256 * columns * count, 32 * 64 * columns * count),
    )(*arrays, own_sum, other_sum, own, other)
    return own_sum, other_sum, totals


def eliminate(matrix, right):
    size = matrix.shape[0]
    work = jnp.concatenate([matrix, right], axis=1)
    rows = lax.broadcasted_iota(jnp.int32, (size, 1), 0)
    pivots = jnp.zeros((size, 1), F32)
    for k in range(size):
        inverse = 1.0 / work[k : k + 1, k : k + 1]
        here = rows == k
        factor = jnp.where(here, 0.0, work[:, k : k + 1] * inverse)
        pivots = jnp.where(here, inverse, pivots)
        work = work - factor * work[k : k + 1, :]
    return work[:, size:] * pivots


def dot32(a, b, dims=(((1,), (0,)), ((), ()))):
    return lax.dot_general(a, b, dims, precision=HIGHEST, preferred_element_type=F32)


def mix_body(gram_ref, lcms_gram_ref, ppm_gram_ref, out_ref):
    rank = lcms_gram_ref.shape[0]
    out_ref[...] = eliminate(gram_ref[:, :rank], lcms_gram_ref[...] + ppm_gram_ref[...])


def mix_pass(gram, lcms_gram, ppm_gram):
    return pl.pallas_call(
        mix_body,
        name="mix_pass",
        out_shape=jax.ShapeDtypeStruct(lcms_gram.shape, F32),
        cost_estimate=cost(1 << 22, 65536),
    )(gram, lcms_gram, ppm_gram)


def sample_body(fit_ref, mix_ref, lcms_gram_ref, lcms_ref, out_ref):
    rank = mix_ref.shape[0]
    mix = mix_ref[...]
    fit = dot32(fit_ref[:, :rank], mix)
    new_gram = dot32(mix, dot32(fit_ref[:, rank:], mix), (((0,), (0,)), ((), ())))
    right = lcms_ref[:, :rank] + fit
    out_ref[...] = eliminate(lcms_gram_ref[...] + new_gram, right.T).T


def sample_pass(fit, mix, lcms_gram, lcms_part):
    return pl.pallas_call(
        sample_body,
        name="sample_pass",
        out_shape=jax.ShapeDtypeStruct((fit.shape[0], mix.shape[0]), F32),
        cost_estimate=cost(1 << 22, 65536),
    )(fit, mix, lcms_gram, lcms_part)


def ppm_body(pieces, chip_ref, mix_ref, *refs):
    out_ref = refs[-1]
    rank, width = mix_ref.shape[0], refs[0].shape[1]
    high, low = split(mix_ref[...].T)
    left = jnp.concatenate(
        [jnp.concatenate([high, high], axis=1), jnp.concatenate([low, low], axis=1)], axis=0
    )
    for piece in range(pieces):
        products = jnp.dot(left, stack_split([refs[piece][...]]), preferred_element_type=F32)
        out_ref[:, piece * width : (piece + 1) * width] = products[:rank] + products[rank:]


def ppm_pass(chip, mix, totals, width):
    rank, pieces = mix.shape[0], len(totals)
    return pl.pallas_call(
        functools.partial(ppm_body, pieces),
        name="ppm_pass",
        grid_spec=pltpu.PrefetchScalarGridSpec(
            num_scalar_prefetch=1,
            grid=(1,),
            in_specs=[whole(mix.shape)]
            + [pl.BlockSpec((rank, width), lambda i, c: (0, c[0])) for _ in totals],
            out_specs=whole((rank, pieces * width)),
        ),
        out_shape=jax.ShapeDtypeStruct((rank, pieces * width), F32),
        cost_estimate=cost(2 * 256 * 128 * pieces * width, 8 * 64 * pieces * width),
    )(chip, mix, *totals)


def sum_over_mz(values, count):
    result = values
    for step in range(1, count):
        result = result + lax.ppermute(values, "mz", [(i, (i + step) % count) for i in range(count)])
    return result


def sum_over_chips(parts, runs):
    lines = [4 * line for line in range(runs // 8)]

    def send(values, pairs):
        hops = [
            (2 * (line + a) + core, 2 * (line + b) + core) for line in lines for a, b in pairs for core in (0, 1)
        ]
        return lax.ppermute(values, "run", hops)

    sweeps = []
    for part in parts:
        inward = send(part, [(0, 1), (3, 2)])
        across = send(part + inward, [(1, 2), (2, 1)])
        outward = send(part + across, [(1, 0), (2, 3)])
        if len(lines) > 1:
            line_total = part + inward + across + outward
            for step in range(1, len(lines)):
                shifted = [(i, (i + 8 * step) % runs) for i in range(runs)]
                part = part + lax.ppermute(line_total, "run", shifted)
        sweeps.append((part, inward, across, outward))
    return sweeps


def per_device(runs, mzs, lcms, spectra, scan_factor, mz_factor, ppm_factor):
    rank = mz_factor.shape[0]
    samples, positions = spectra.shape
    blocks = runs // 2
    width = positions // runs
    pieces = min(8, width // 128)
    run = lax.axis_index("run").astype(jnp.int32)
    core, chip = (run % 2).reshape(1), (run // 2).reshape(1)
    swap = [(i, i ^ 1) for i in range(runs)]

    early, own, leaving = nmr_pass(core, spectra, ppm_factor, mz_factor, blocks, pieces)
    other = lax.ppermute(leaving, "run", swap)
    early = sum_over_mz(early, mzs)
    lcms_part = sum_over_mz(lcms_pass(lcms, scan_factor, mz_factor), mzs)
    scan_gram = jnp.dot(scan_factor, scan_factor.T, precision=HIGHEST)
    lcms_gram = scan_gram * early[rank:, :rank]
    ppm_gram = early[:rank, rank:]
    own_rows = lcms_part[:, :rank] + early[:rank, :rank]
    other_rows = lax.ppermute(own_rows, "run", swap)
    left, gram = weights_pass(own_rows, other_rows)
    parts = project_pass(left, own, other, gram, 0, 1) + project_pass(left, own, other, None, 1, pieces - 1)
    sweeps = sum_over_chips(parts, runs)
    totals = []
    own_sum = other_sum = jnp.zeros((samples, 2 * rank), F32)
    for k in range(0, pieces, 2):
        own_sum, other_sum, done = fit_pass(sweeps[k : k + 2], own_sum, other_sum, own, other, k)
        totals += done
    mix = mix_pass(sum(array[:, own.shape[2] :] for array in sweeps[0]), lcms_gram, ppm_gram)
    ppm_new = ppm_pass(chip, mix, totals, width // pieces)
    fit = sum_over_mz(own_sum + lax.ppermute(other_sum, "run", swap), mzs)
    sample_factor = sample_pass(fit, mix, lcms_gram, lcms_part)
    return (sample_factor, ppm_new)


def solution(mesh):
    runs, mzs = mesh.shape["run"], mesh.shape["mz"]

    def whole_step(lcms, spectra, scan_factor, mz_factor, ppm_factor):
        return per_device(runs, mzs, lcms, spectra, scan_factor, mz_factor, ppm_factor)

    return jax.shard_map(
        whole_step,
        mesh=mesh,
        in_specs=(P("run", None, "mz"), P("run", "mz"), P(), P(None, "mz"), P(None, "mz")),
        out_specs=(P("run", None), P(None, ("mz", "run"))),
        check_vma=False,
    )
```

```python
import functools

import jax
import jax.numpy as jnp
from jax import lax
from jax.experimental import pallas as pl
from jax.experimental.pallas import tpu as pltpu
from jax.sharding import PartitionSpec as P


F32, BF16 = jnp.float32, jnp.bfloat16
HIGHEST = lax.Precision.HIGHEST
NT = (((1,), (1,)), ((), ()))


def split(values):
    high = values.astype(BF16)
    return high, (values - high.astype(F32)).astype(BF16)


def stack_split(blocks):
    pairs = [split(block) for block in blocks]
    return jnp.concatenate([pair[0] for pair in pairs] + [pair[1] for pair in pairs], axis=0)


def cost(flops, transferred):
    return pl.CostEstimate(flops=int(flops), bytes_accessed=int(transferred), transcendentals=0)


def whole(shape):
    return pl.BlockSpec(shape, lambda *_: (0,) * len(shape))


def nmr_body(blocks, swept, core_ref, chip_ref, *refs):
    spectra_refs, ppm_refs = refs[: 2 * blocks], refs[2 * blocks : 4 * blocks]
    mz_ref, part_ref, keep_ref, send_ref, *parcels = refs[4 * blocks : -1]
    total = refs[-1]
    piece = pl.program_id(0)
    rank = mz_ref.shape[0]

    @pl.when(piece == 0)
    def _():
        total[...] = jnp.zeros_like(total)
        channels = stack_split([mz_ref[...]])
        products = lax.dot_general(channels, channels, NT, preferred_element_type=F32)
        rows = products[:rank] + products[rank:]
        part_ref[:, rank:] = jnp.zeros_like(part_ref[:, rank:])
        part_ref[rank:, rank:] = rows[:, :rank] + rows[:, rank:]

    halves = [
        jnp.concatenate([spectra_refs[2 * b + core][...] for b in range(blocks)], axis=1) for core in (0, 1)
    ]
    values = jnp.concatenate(halves, axis=1)
    positions = stack_split([jnp.concatenate([ref[...] for core in (0, 1) for ref in ppm_refs[core::2]], axis=1)])
    left = jnp.concatenate([stack_split([values]), positions[:rank]], axis=0)
    total[...] += lax.dot_general(left, positions, NT, preferred_element_type=F32)

    for core in (0, 1):

        @pl.when(core_ref[0] == core)
        def _():
            keep_ref[0] = halves[core]
            send_ref[0] = halves[1 - core]

    if parcels:
        width = parcels[0].shape[3]

        @pl.when(piece >= swept)
        def _():
            for step, parcel in enumerate(parcels, 1):
                columns = pl.ds(pl.multiple_of((chip_ref[0] ^ step) * width, width), width)
                parcel[0, 0] = keep_ref[0, :, columns]
                parcel[0, 1] = send_ref[0, :, columns]

    @pl.when(piece == pl.num_programs(0) - 1)
    def _():
        samples = spectra_refs[0].shape[0]
        products = total[...]
        fit = products[:samples] + products[samples : 2 * samples]
        gram = products[2 * samples :]
        mixed = gram[:, rank:]
        part_ref[:rank, :rank] = fit[:, :rank] + fit[:, rank:]
        part_ref[rank:, :rank] = gram[:, :rank] + (mixed + mixed.T)


def nmr_pass(core, chip, spectra, ppm_factor, mz_factor, blocks, pieces, swept):
    samples, positions = spectra.shape
    rank, channels = mz_factor.shape
    width = positions // (2 * blocks * pieces)

    def columns(rows):
        return [
            pl.BlockSpec((rows, width), functools.partial(lambda b, k, c, h: (0, b * pieces + k), b))
            for b in range(2 * blocks)
        ]

    sorted_shape = jax.ShapeDtypeStruct((pieces, samples, blocks * width), F32)
    parcels = blocks - 1 if swept < pieces else 0
    parcel_shape = jax.ShapeDtypeStruct((pieces - swept, 2, samples, width), F32)
    return pl.pallas_call(
        functools.partial(nmr_body, blocks, swept),
        name="nmr_pass",
        grid_spec=pltpu.PrefetchScalarGridSpec(
            num_scalar_prefetch=2,
            grid=(pieces,),
            in_specs=columns(samples) + columns(rank) + [whole((rank, channels))],
            out_specs=[whole((2 * rank, 2 * rank))]
            + [pl.BlockSpec((1, samples, blocks * width), lambda k, c, h: (k, 0, 0))] * 2
            + [pl.BlockSpec((1, 2, samples, width), lambda k, c, h: (jnp.maximum(k - swept, 0), 0, 0, 0))] * parcels,
            scratch_shapes=[pltpu.VMEM((2 * samples + rank, 2 * rank), F32)],
        ),
        out_shape=[jax.ShapeDtypeStruct((2 * rank, 2 * rank), F32), sorted_shape, sorted_shape]
        + [parcel_shape] * parcels,
        cost_estimate=cost(2 * 256 * 256 * positions, 4 * 3 * 64 * positions),
    )(core, chip, *([spectra] * (2 * blocks)), *([ppm_factor] * (2 * blocks)), mz_factor)


def lcms_body(lcms_ref, scan_ref, mz_ref, part_ref, out_ref, weights, scans):
    rank = mz_ref.shape[0]
    step = pl.program_id(0)
    count, steps, channels = lcms_ref.shape

    @pl.when(step == 0)
    def _():
        high, low = split(mz_ref[...].T)
        weights[...] = jnp.concatenate([high, low], axis=1)
        scan = scan_ref[...].astype(BF16).astype(F32).T
        scans[...] = jnp.concatenate([scan, scan], axis=1)
        out_ref[rank:, :] = part_ref[rank:, :]

    inner = jnp.dot(
        lcms_ref[...].reshape(count * steps, channels), weights[...], preferred_element_type=F32
    )
    sums = jnp.sum(inner.reshape(count, steps, 2 * rank) * scans[...][None], axis=1)
    rows = pl.ds(pl.multiple_of(step * count, count), count)
    out_ref[rows, :] = sums + pltpu.roll(sums, rank, 1) + part_ref[rows, :]


def lcms_pass(lcms, scan_factor, mz_factor, part):
    samples, steps, channels = lcms.shape
    rank = mz_factor.shape[0]
    count = 8
    return pl.pallas_call(
        lcms_body,
        name="lcms_pass",
        grid=(samples // count,),
        in_specs=[
            pl.BlockSpec((count, steps, channels), lambda i: (i, 0, 0)),
            whole(scan_factor.shape),
            whole(mz_factor.shape),
            whole(part.shape),
        ],
        out_specs=whole(part.shape),
        out_shape=jax.ShapeDtypeStruct(part.shape, F32),
        scratch_shapes=[
            pltpu.VMEM((channels, 2 * rank), BF16),
            pltpu.VMEM((steps, 2 * rank), F32),
        ],
        cost_estimate=cost(2 * samples * steps * channels * 256, 2 * samples * steps * channels),
    )(lcms, scan_factor, mz_factor, part)


def first_body(own_pack, other_pack, own_ref, other_ref, left_ref, rows_ref, out_ref):
    rank, columns = rows_ref.shape[1] // 2, own_ref.shape[2]
    samples = own_ref.shape[1]
    rows = jnp.concatenate([own_pack[:samples, :rank], other_pack[:samples, :rank]], axis=1)
    rows_ref[...] = rows
    left = wide_rows(rows)
    left_ref[...] = left
    sides = [(own_ref[0], other_ref[0], 0), (rows[:, :rank], rows[:, rank:], columns)]
    for own, other, start in sides:
        products = jnp.dot(left, stack_split([own, other]), preferred_element_type=F32)
        out_ref[:, start : start + own.shape[1]] = products[:rank] + products[rank:]
    out_ref[:, columns + rank :] = jnp.zeros_like(out_ref[:, columns + rank :])


def wide_rows(rows):
    rank = rows.shape[1] // 2
    turned = rows.T
    return jnp.concatenate(
        [
            jnp.concatenate([part[:rank], part[rank:], part[:rank], part[rank:]], axis=1)
            for part in split(turned)
        ],
        axis=0,
    )


def first_pass(own_pack, other_pack, own, other):
    _, samples, columns = own.shape
    rank = own_pack.shape[1] // 2
    piece = pl.BlockSpec((1, samples, columns), lambda k: (0, 0, 0))
    return pl.pallas_call(
        first_body,
        name="first_pass",
        grid=(1,),
        in_specs=[whole(own_pack.shape)] * 2 + [piece] * 2,
        out_specs=[
            whole((2 * rank, 4 * samples)),
            whole((samples, 2 * rank)),
            whole((rank, columns + 2 * rank)),
        ],
        out_shape=[
            jax.ShapeDtypeStruct((2 * rank, 4 * samples), BF16),
            jax.ShapeDtypeStruct((samples, 2 * rank), F32),
            pltpu.VMEM((rank, columns + 2 * rank), F32),
        ],
        cost_estimate=cost(2 * 256 * 256 * columns, 12 * 64 * columns),
    )(own_pack, other_pack, own, other)


def project_body(left_ref, own_ref, other_ref, *outs):
    rank = left_ref.shape[0] // 2
    right = stack_split([own_ref[0], other_ref[0]])
    products = jnp.dot(left_ref[...], right, preferred_element_type=F32)
    values = products[:rank] + products[rank:]
    for k, out_ref in enumerate(outs):

        @pl.when(pl.program_id(0) == k)
        def _():
            out_ref[...] = values


def project_pass(left, own, other, first, count):
    _, samples, columns = own.shape
    rank = left.shape[0] // 2
    piece = pl.BlockSpec((1, samples, columns), lambda k: (first + k, 0, 0))
    return pl.pallas_call(
        project_body,
        name="project_pass",
        grid=(count,),
        in_specs=[whole(left.shape), piece, piece],
        out_specs=[whole((rank, columns))] * count,
        out_shape=[pltpu.VMEM((rank, columns), F32)] * count,
        cost_estimate=cost(2 * 256 * 256 * columns * count, 12 * 64 * columns * count),
    )(left, own, other)


def fit_body(count, earlier, *refs):
    sweeps, refs = refs[: 4 * count], refs[4 * count :]
    own_ref, other_ref, sums_ref = refs[0], refs[1], refs[2 + earlier]
    _, samples, _ = own_ref.shape
    rank = sums_ref.shape[2] // 2
    sums = None
    for k in range(count):
        part, inward, across, outward = (ref[...] for ref in sweeps[4 * k : 4 * k + 4])
        total = part + inward + across + outward
        refs[3 + earlier + k][...] = total
        right = stack_split([total])
        rows = jnp.concatenate([stack_split([own_ref[k], other_ref[k]]), right], axis=0)
        products = lax.dot_general(rows, right, NT, preferred_element_type=F32)
        sums = products if sums is None else sums + products
    sums = sums[:, :rank] + sums[:, rank:]
    gram = sums[4 * samples : 4 * samples + rank] + sums[4 * samples + rank :]
    for side in (0, 1):
        fit = sums[side * samples : (side + 1) * samples] + sums[(side + 2) * samples : (side + 3) * samples]
        total = jnp.concatenate([fit, gram], axis=1)
        for ref in refs[2 : 2 + earlier]:
            total = total + ref[side]
        sums_ref[side] = total


def fit_pass(sweeps, earlier, own, other, first):
    _, samples, columns = own.shape
    count, rank = len(sweeps), sweeps[0][0].shape[0]
    pieces = pl.BlockSpec((count, samples, columns), lambda i: (first // count, 0, 0))
    assert first % count == 0
    arrays = [array for sweep in sweeps for array in sweep]
    sums_shape = (2, samples, 2 * rank)
    sums, *totals = pl.pallas_call(
        functools.partial(fit_body, count, len(earlier)),
        grid=(1,),
        in_specs=[whole((rank, columns))] * len(arrays)
        + [pieces, pieces]
        + [whole(sums_shape)] * len(earlier),
        out_specs=[whole(sums_shape)] + [whole((rank, columns))] * count,
        out_shape=[jax.ShapeDtypeStruct(sums_shape, F32)]
        + [jax.ShapeDtypeStruct((rank, columns), F32)] * count,
        cost_estimate=cost(2 * 384 * 256 * columns * count, 32 * 64 * columns * count),
    )(*arrays, own, other, *earlier)
    return sums, totals


def eliminate(matrix, right):
    size, ahead = matrix.shape[0], 4
    whole_rows = jnp.concatenate([matrix, right], axis=1)
    groups = [whole_rows[i : i + 8] for i in range(0, size, 8)]
    lanes = whole_rows.shape[1]
    sublane = lax.broadcasted_iota(jnp.int32, (8, lanes), 0)

    def reduce(targets, columns, home, place, inverse):
        row = jnp.broadcast_to(targets[home][place : place + 1], (8, lanes)) * inverse
        reduced = [target - column * row for target, column in zip(targets, columns)]
        reduced[home] = jnp.where(sublane == place, row, reduced[home])
        return reduced

    for base in range(0, size, ahead):
        spread = [
            [jnp.broadcast_to(group[:, k : k + 1], (8, lanes)) for group in groups]
            for k in range(base, base + ahead)
        ]
        for j in range(ahead):
            home, place = divmod(base + j, 8)
            inverse = 1.0 / jnp.broadcast_to(spread[j][home][place : place + 1], (8, lanes))
            for i in range(j + 1, ahead):
                spread[i] = reduce(spread[i], spread[j], home, place, inverse)
            groups = reduce(groups, spread[j], home, place, inverse)
    return jnp.concatenate(groups, axis=0)[:, size:]


def dot32(a, b, dims=(((1,), (0,)), ((), ()))):
    return lax.dot_general(a, b, dims, precision=HIGHEST, preferred_element_type=F32)


def mix_body(*refs):
    parts, (pack_ref, scan_ref, out_ref, lcms_gram_ref) = refs[:-4], refs[-4:]
    rank = out_ref.shape[0]
    scan = scan_ref[...]
    lcms_gram = dot32(scan, scan, NT) * pack_ref[rank:, rank:]
    lcms_gram_ref[...] = lcms_gram
    gram = sum(part[...] for part in parts)
    out_ref[...] = eliminate(gram[:, :rank], lcms_gram + pack_ref[rank:, :rank])


def mix_pass(sweep, pack, scan_factor, columns):
    rank = scan_factor.shape[0]
    shape = jax.ShapeDtypeStruct((rank, rank), F32)
    return pl.pallas_call(
        mix_body,
        name="mix_pass",
        grid=(1,),
        in_specs=[pl.BlockSpec((rank, 2 * rank), lambda i: (0, columns // (2 * rank)))] * len(sweep)
        + [whole(pack.shape), whole(scan_factor.shape)],
        out_specs=[whole(shape.shape)] * 2,
        out_shape=[shape, shape],
        cost_estimate=cost(1 << 22, 65536),
    )(*sweep, pack, scan_factor)


def sample_body(fit_ref, mix_ref, lcms_gram_ref, pack_ref, out_ref):
    rank = mix_ref.shape[0]
    mix = mix_ref[...]
    fit = dot32(fit_ref[:, :rank], mix)
    new_gram = dot32(mix, dot32(fit_ref[:, rank:], mix), (((0,), (0,)), ((), ())))
    right = pack_ref[: fit.shape[0], rank:] + fit
    out_ref[...] = eliminate(lcms_gram_ref[...] + new_gram, right.T).T


def sample_pass(fit, mix, lcms_gram, pack):
    return pl.pallas_call(
        sample_body,
        name="sample_pass",
        out_shape=jax.ShapeDtypeStruct((fit.shape[0], mix.shape[0]), F32),
        cost_estimate=cost(1 << 22, 65536),
    )(fit, mix, lcms_gram, pack)


def ppm_body(chip_ref, mix_ref, *refs):
    out_ref = refs[-1]
    rank = mix_ref.shape[0]
    high, low = split(mix_ref[...].T)
    left = jnp.concatenate(
        [jnp.concatenate([high, high], axis=1), jnp.concatenate([low, low], axis=1)], axis=0
    )
    start = 0
    for ref in refs[:-1]:
        products = jnp.dot(left, stack_split([ref[...]]), preferred_element_type=F32)
        out_ref[:, start : start + ref.shape[1]] = products[:rank] + products[rank:]
        start += ref.shape[1]


def ppm_pass(chip, mix, totals, direct, width):
    rank, pieces = mix.shape[0], len(totals)
    directs = [] if direct is None else [direct]
    columns = pieces * width + sum(d.shape[1] for d in directs)
    return pl.pallas_call(
        ppm_body,
        name="ppm_pass",
        grid_spec=pltpu.PrefetchScalarGridSpec(
            num_scalar_prefetch=1,
            grid=(1,),
            in_specs=[whole(mix.shape)]
            + [pl.BlockSpec((rank, width), lambda i, c: (0, c[0])) for _ in totals]
            + [whole(d.shape) for d in directs],
            out_specs=whole((rank, columns)),
        ),
        out_shape=jax.ShapeDtypeStruct((rank, columns), F32),
        cost_estimate=cost(2 * 256 * 128 * columns, 8 * 64 * columns),
    )(chip, mix, *totals, *directs)


def direct_body(chips, count, chip_ref, *refs):
    rows, refs = refs[:chips], refs[chips:]
    own, other, refs = refs[:count], refs[count : 2 * count], refs[2 * count :]
    came, swapped, projected_ref, sums_refs = refs[: chips - 1], refs[chips - 1 : 2 * chips - 2], refs[2 * chips - 2], refs[2 * chips - 1 :]
    samples, width = own[0].shape[1:]
    rank = rows[0].shape[1] // 2
    left = [wide_rows(pair[...]) for pair in rows]
    sums = [None] * chips
    gram = None
    for j in range(count):
        stacks = [stack_split([own[j][0], other[j][0]])] + [
            stack_split([came[x][j, 0], swapped[x][j, 0]]) for x in range(chips - 1)
        ]
        products = sum(
            jnp.dot(left[x], stacks[x], preferred_element_type=F32) for x in range(chips)
        )
        values = products[:rank] + products[rank:]
        projected_ref[:, j * width : (j + 1) * width] = values
        right = stack_split([values])
        for x in range(chips):
            fit = lax.dot_general(stacks[x], right, NT, preferred_element_type=F32)
            sums[x] = fit if j == 0 else sums[x] + fit
        square = lax.dot_general(right, right, NT, preferred_element_type=F32)
        gram = square if j == 0 else gram + square
    gram = gram[:rank] + gram[rank:]
    gram = gram[:, :rank] + gram[:, rank:]
    for x in range(chips):
        fit = sums[x][: 2 * samples] + sums[x][2 * samples :]
        fit = fit[:, :rank] + fit[:, rank:]
        for side in (0, 1):
            sums_refs[x][side] = jnp.concatenate([fit[side * samples : (side + 1) * samples], gram], axis=1)


def direct_pass(chip, rows, own, other, came, swapped, first):
    chips, count = len(rows), own.shape[0] - first
    samples, rank = own.shape[1], rows[0].shape[1] // 2
    width = came[0].shape[3]
    pieces = [
        pl.BlockSpec((1, samples, width), functools.partial(lambda j, i, c: (first + j, 0, c[0]), j))
        for j in range(count)
    ]
    return pl.pallas_call(
        functools.partial(direct_body, chips, count),
        name="direct_pass",
        grid_spec=pltpu.PrefetchScalarGridSpec(
            num_scalar_prefetch=1,
            grid=(1,),
            in_specs=[whole(r.shape) for r in rows]
            + pieces
            + pieces
            + [pl.BlockSpec((count, 1, samples, width), lambda i, c: (0, 0, 0, 0))] * (chips - 1)
            + [pl.BlockSpec((count, 1, samples, width), lambda i, c: (0, 1, 0, 0))] * (chips - 1),
            out_specs=[whole((rank, count * width))] + [whole((2, samples, 2 * rank))] * chips,
        ),
        out_shape=[jax.ShapeDtypeStruct((rank, count * width), F32)]
        + [jax.ShapeDtypeStruct((2, samples, 2 * rank), F32)] * chips,
        cost_estimate=cost(2 * 512 * 512 * count * width * 2, 4 * 512 * count * width),
    )(chip, *rows, *([own] * count), *([other] * count), *came, *swapped)


def sum_over_mz(values, count):
    result = values
    for step in range(1, count):
        hops = [(i, (i + step) % count) for i in range(count)]
        result = result + lax.ppermute(values, "mz", hops)
    return result


def from_chips(values, runs):
    chips = runs // 2
    return [
        lax.ppermute(values[step - 1], "run", [(i, i ^ (2 * step)) for i in range(runs)])
        for step in range(1, chips)
    ]


def sum_over_chips(parts, runs):
    lines = [4 * line for line in range(runs // 8)]

    def send(values, pairs):
        hops = [
            (2 * (line + a) + core, 2 * (line + b) + core) for line in lines for a, b in pairs for core in (0, 1)
        ]
        return lax.ppermute(values, "run", hops)

    sweeps = []
    for part in parts:
        inward = send(part, [(0, 1), (3, 2)])
        across = send(part + inward, [(1, 2), (2, 1)])
        outward = send(part + across, [(1, 0), (2, 3)])
        if len(lines) > 1:
            line_total = part + inward + across + outward
            for step in range(1, len(lines)):
                shifted = [(i, (i + 8 * step) % runs) for i in range(runs)]
                part = part + lax.ppermute(line_total, "run", shifted)
        sweeps.append((part, inward, across, outward))
    return sweeps


def per_device(runs, mzs, lcms, spectra, scan_factor, mz_factor, ppm_factor):
    _, positions = spectra.shape
    chips = runs // 2
    width = positions // runs
    pieces = min(8, width // 128)
    swept = pieces // 2 if chips == 4 else pieces
    width = width // pieces
    run = lax.axis_index("run").astype(jnp.int32)
    core, chip = (run % 2).reshape(1), (run // 2).reshape(1)
    swap = [(i, i ^ 1) for i in range(runs)]

    part, own, leaving, *parcels = nmr_pass(core, chip, spectra, ppm_factor, mz_factor, chips, pieces, swept)
    came = from_chips(parcels, runs) if parcels else []
    other = lax.ppermute(leaving, "run", swap)
    pack = lcms_pass(lcms, scan_factor, mz_factor, part)
    pack = sum_over_mz(pack, mzs)
    left, rows, first = first_pass(pack, lax.ppermute(pack, "run", swap), own, other)
    sweeps = sum_over_chips([first, *project_pass(left, own, other, 1, swept - 1)], runs)
    projected, direct = None, []
    if parcels:
        rows = [rows] + from_chips([rows] * (chips - 1), runs)
        swapped = [lax.ppermute(array, "run", swap) for array in came]
        projected, *sums = direct_pass(chip, rows, own, other, came, swapped, swept)
        direct = sums[:1] + from_chips(sums[1:], runs)
    totals, sums = [], []
    for k in range(0, swept, 2):
        earlier = sums + (direct if k + 2 == swept else [])
        sums, done = fit_pass(sweeps[k : k + 2], earlier, own, other, k)
        totals, sums = totals + done, [sums]
    mix, lcms_gram = mix_pass(sweeps[0], pack, scan_factor, own.shape[2])
    ppm_new = ppm_pass(chip, mix, totals, projected, width)
    fit = sum_over_mz(sums[0][0] + lax.ppermute(sums[0], "run", swap)[1], mzs)
    sample_factor = sample_pass(fit, mix, lcms_gram, pack)
    return (sample_factor, ppm_new)


def solution(mesh):
    runs, mzs = mesh.shape["run"], mesh.shape["mz"]

    def whole_step(lcms, spectra, scan_factor, mz_factor, ppm_factor):
        return per_device(runs, mzs, lcms, spectra, scan_factor, mz_factor, ppm_factor)

    return jax.shard_map(
        whole_step,
        mesh=mesh,
        in_specs=(P("run", None, "mz"), P("run", "mz"), P(), P(None, "mz"), P(None, "mz")),
        out_specs=(P("run", None), P(None, ("mz", "run"))),
        check_vma=False,
    )
```

```python
import functools

import jax
import jax.numpy as jnp
from jax import lax
from jax.experimental import pallas as pl
from jax.experimental.pallas import tpu as pltpu
from jax.sharding import PartitionSpec as P


F32, BF16 = jnp.float32, jnp.bfloat16
HIGHEST = lax.Precision.HIGHEST
NT = (((1,), (1,)), ((), ()))


def split(values):
    high = values.astype(BF16)
    return high, (values - high.astype(F32)).astype(BF16)


def stack_split(blocks):
    pairs = [split(block) for block in blocks]
    return jnp.concatenate([pair[0] for pair in pairs] + [pair[1] for pair in pairs], axis=0)


def cost(flops, transferred):
    return pl.CostEstimate(flops=int(flops), bytes_accessed=int(transferred), transcendentals=0)


def within(mebibytes):
    return pltpu.CompilerParams(vmem_limit_bytes=mebibytes << 20)


def in_vmem(array):
    return pltpu.with_memory_space_constraint(array, pltpu.VMEM)


def whole(shape):
    return pl.BlockSpec(shape, lambda *_: (0,) * len(shape))


def sort_body(blocks, swept, core_ref, chip_ref, *refs):
    spectra_refs, (keep_ref, send_ref, *parcels) = refs[: 2 * blocks], refs[2 * blocks :]
    width = spectra_refs[0].shape[1]
    for core in (0, 1):

        @pl.when(core_ref[0] == core)
        def _():
            for b in range(blocks):
                keep_ref[0, :, b * width : (b + 1) * width] = spectra_refs[2 * b + core][...]
                send_ref[0, :, b * width : (b + 1) * width] = spectra_refs[2 * b + 1 - core][...]

    if parcels:

        @pl.when(pl.program_id(0) >= swept)
        def _():
            for step, parcel in enumerate(parcels, 1):
                columns = pl.ds(pl.multiple_of((chip_ref[0] ^ step) * width, width), width)
                parcel[0, 0] = keep_ref[0, :, columns]
                parcel[0, 1] = send_ref[0, :, columns]


def sort_pass(core, chip, spectra, blocks, pieces, swept):
    samples, positions = spectra.shape
    width = positions // (2 * blocks * pieces)
    columns = [
        pl.BlockSpec((samples, width), functools.partial(lambda b, k, c, h: (0, b * pieces + k), b))
        for b in range(2 * blocks)
    ]
    sorted_shape = jax.ShapeDtypeStruct((pieces, samples, blocks * width), F32)
    parcels = blocks - 1 if swept < pieces else 0
    parcel_shape = jax.ShapeDtypeStruct((pieces - swept, 2, samples, width), F32)
    return pl.pallas_call(
        functools.partial(sort_body, blocks, swept),
        name="sort_pass",
        compiler_params=within(12),
        grid_spec=pltpu.PrefetchScalarGridSpec(
            num_scalar_prefetch=2,
            grid=(pieces,),
            in_specs=columns,
            out_specs=[pl.BlockSpec((1, samples, blocks * width), lambda k, c, h: (k, 0, 0))] * 2
            + [pl.BlockSpec((1, 2, samples, width), lambda k, c, h: (jnp.maximum(k - swept, 0), 0, 0, 0))] * parcels,
        ),
        out_shape=[sorted_shape, sorted_shape] + [parcel_shape] * parcels,
        cost_estimate=cost(1 << 20, 4 * 2 * 64 * positions),
    )(core, chip, *([spectra] * (2 * blocks)))


def nmr_body(blocks, core_ref, keep_ref, send_ref, *refs):
    ppm_refs, (mz_ref, part_ref, total) = refs[: 2 * blocks], refs[2 * blocks :]
    piece = pl.program_id(0)
    rank = mz_ref.shape[0]

    @pl.when(piece == 0)
    def _():
        total[...] = jnp.zeros_like(total)
        channels = stack_split([mz_ref[...]])
        products = lax.dot_general(channels, channels, NT, preferred_element_type=F32)
        rows = products[:rank] + products[rank:]
        part_ref[:, rank:] = jnp.zeros_like(part_ref[:, rank:])
        part_ref[rank:, rank:] = rows[:, :rank] + rows[:, rank:]

    values = jnp.concatenate([keep_ref[0], send_ref[0]], axis=1)
    positions = stack_split([jnp.concatenate([ref[...] for ref in ppm_refs], axis=1)])
    left = jnp.concatenate([stack_split([values]), positions[:rank]], axis=0)
    total[...] += lax.dot_general(left, positions, NT, preferred_element_type=F32)

    @pl.when(piece == pl.num_programs(0) - 1)
    def _():
        samples = keep_ref.shape[1]
        products = total[...]
        fit = products[:samples] + products[samples : 2 * samples]
        gram = products[2 * samples :]
        mixed = gram[:, rank:]
        part_ref[:rank, :rank] = fit[:, :rank] + fit[:, rank:]
        part_ref[rank:, :rank] = gram[:, :rank] + (mixed + mixed.T)


def nmr_pass(core, keep, send, ppm_factor, mz_factor, blocks):
    pieces, samples, columns = keep.shape
    rank, channels = mz_factor.shape
    width = columns // blocks

    def positions(side):
        return [
            pl.BlockSpec(
                (rank, width),
                functools.partial(lambda b, k, c: (0, (2 * b + (c[0] ^ side)) * pieces + k), b),
            )
            for b in range(blocks)
        ]

    piece = pl.BlockSpec((1, samples, columns), lambda k, c: (k, 0, 0))
    return pl.pallas_call(
        functools.partial(nmr_body, blocks),
        name="nmr_pass",
        compiler_params=within(16),
        grid_spec=pltpu.PrefetchScalarGridSpec(
            num_scalar_prefetch=1,
            grid=(pieces,),
            in_specs=[piece, piece] + positions(0) + positions(1) + [whole((rank, channels))],
            out_specs=whole((2 * rank, 2 * rank)),
            scratch_shapes=[pltpu.VMEM((2 * samples + rank, 2 * rank), F32)],
        ),
        out_shape=jax.ShapeDtypeStruct((2 * rank, 2 * rank), F32),
        cost_estimate=cost(2 * 256 * 256 * pieces * columns, 4 * 3 * 64 * pieces * columns),
    )(core, keep, send, *([ppm_factor] * (2 * blocks)), mz_factor)


def lcms_body(lcms_ref, scan_ref, mz_ref, part_ref, out_ref, weights, scans):
    rank = mz_ref.shape[0]
    step = pl.program_id(0)
    count, steps, channels = lcms_ref.shape

    @pl.when(step == 0)
    def _():
        high, low = split(mz_ref[...].T)
        weights[...] = jnp.concatenate([high, low], axis=1)
        scan = scan_ref[...].astype(BF16).astype(F32).T
        scans[...] = jnp.concatenate([scan, scan], axis=1)
        out_ref[rank:, :] = part_ref[rank:, :]

    inner = jnp.dot(
        lcms_ref[...].reshape(count * steps, channels), weights[...], preferred_element_type=F32
    )
    sums = jnp.sum(inner.reshape(count, steps, 2 * rank) * scans[...][None], axis=1)
    rows = pl.ds(pl.multiple_of(step * count, count), count)
    out_ref[rows, :] = sums + pltpu.roll(sums, rank, 1) + part_ref[rows, :]


def lcms_pass(lcms, scan_factor, mz_factor, part):
    samples, steps, channels = lcms.shape
    rank = mz_factor.shape[0]
    count = 8
    return pl.pallas_call(
        lcms_body,
        name="lcms_pass",
        compiler_params=within(32),
        grid=(samples // count,),
        in_specs=[
            pl.BlockSpec((count, steps, channels), lambda i: (i, 0, 0)),
            whole(scan_factor.shape),
            whole(mz_factor.shape),
            whole(part.shape),
        ],
        out_specs=whole(part.shape),
        out_shape=jax.ShapeDtypeStruct(part.shape, F32),
        scratch_shapes=[
            pltpu.VMEM((channels, 2 * rank), BF16),
            pltpu.VMEM((steps, 2 * rank), F32),
        ],
        cost_estimate=cost(2 * samples * steps * channels * 256, 2 * samples * steps * channels),
    )(lcms, scan_factor, mz_factor, part)


def first_body(own_pack, other_pack, own_ref, other_ref, left_ref, rows_ref, out_ref):
    rank, columns = rows_ref.shape[1] // 2, own_ref.shape[2]
    samples = own_ref.shape[1]
    rows = jnp.concatenate([own_pack[:samples, :rank], other_pack[:samples, :rank]], axis=1)
    rows_ref[...] = rows
    left = wide_rows(rows)
    left_ref[...] = left
    sides = [(own_ref[0], other_ref[0], 0), (rows[:, :rank], rows[:, rank:], columns)]
    for own, other, start in sides:
        products = jnp.dot(left, stack_split([own, other]), preferred_element_type=F32)
        out_ref[:, start : start + own.shape[1]] = products[:rank] + products[rank:]
    out_ref[:, columns + rank :] = jnp.zeros_like(out_ref[:, columns + rank :])


def wide_rows(rows):
    rank = rows.shape[1] // 2
    turned = rows.T
    return jnp.concatenate(
        [
            jnp.concatenate([part[:rank], part[rank:], part[:rank], part[rank:]], axis=1)
            for part in split(turned)
        ],
        axis=0,
    )


def first_pass(own_pack, other_pack, own, other):
    _, samples, columns = own.shape
    rank = own_pack.shape[1] // 2
    piece = pl.BlockSpec((1, samples, columns), lambda k: (0, 0, 0))
    return pl.pallas_call(
        first_body,
        name="first_pass",
        compiler_params=within(12),
        grid=(1,),
        in_specs=[whole(own_pack.shape)] * 2 + [piece] * 2,
        out_specs=[
            whole((2 * rank, 4 * samples)),
            whole((samples, 2 * rank)),
            whole((rank, columns + 2 * rank)),
        ],
        out_shape=[
            jax.ShapeDtypeStruct((2 * rank, 4 * samples), BF16),
            jax.ShapeDtypeStruct((samples, 2 * rank), F32),
            pltpu.VMEM((rank, columns + 2 * rank), F32),
        ],
        cost_estimate=cost(2 * 256 * 256 * columns, 12 * 64 * columns),
    )(own_pack, other_pack, own, other)


def project_body(left_ref, own_ref, other_ref, *outs):
    rank = left_ref.shape[0] // 2
    right = stack_split([own_ref[0], other_ref[0]])
    products = jnp.dot(left_ref[...], right, preferred_element_type=F32)
    values = products[:rank] + products[rank:]
    for k, out_ref in enumerate(outs):

        @pl.when(pl.program_id(0) == k)
        def _():
            out_ref[...] = values


def project_pass(left, own, other, first, count):
    _, samples, columns = own.shape
    rank = left.shape[0] // 2
    piece = pl.BlockSpec((1, samples, columns), lambda k: (first + k, 0, 0))
    return pl.pallas_call(
        project_body,
        name="project_pass",
        compiler_params=within(12),
        grid=(count,),
        in_specs=[whole(left.shape), piece, piece],
        out_specs=[whole((rank, columns))] * count,
        out_shape=[pltpu.VMEM((rank, columns), F32)] * count,
        cost_estimate=cost(2 * 256 * 256 * columns * count, 12 * 64 * columns * count),
    )(left, own, other)


def fit_body(count, earlier, *refs):
    sweeps, refs = refs[: 4 * count], refs[4 * count :]
    own_ref, other_ref, sums_ref = refs[0], refs[1], refs[2 + earlier]
    _, samples, columns = own_ref.shape
    rank = sums_ref.shape[2] // 2
    sums = None
    for k in range(count):
        part, inward, across, outward = (ref[:, :columns] for ref in sweeps[4 * k : 4 * k + 4])
        total = part + inward + across + outward
        refs[3 + earlier + k][...] = total
        right = stack_split([total])
        rows = jnp.concatenate([stack_split([own_ref[k], other_ref[k]]), right], axis=0)
        products = lax.dot_general(rows, right, NT, preferred_element_type=F32)
        sums = products if sums is None else sums + products
    sums = sums[:, :rank] + sums[:, rank:]
    gram = sums[4 * samples : 4 * samples + rank] + sums[4 * samples + rank :]
    for side in (0, 1):
        fit = sums[side * samples : (side + 1) * samples] + sums[(side + 2) * samples : (side + 3) * samples]
        total = jnp.concatenate([fit, gram], axis=1)
        for ref in refs[2 : 2 + earlier]:
            total = total + ref[side]
        sums_ref[side] = total


def fit_pass(sweeps, earlier, own, other, first):
    _, samples, columns = own.shape
    count, rank = len(sweeps), sweeps[0][0].shape[0]
    pieces = pl.BlockSpec((count, samples, columns), lambda i: (first // count, 0, 0))
    assert first % count == 0
    arrays = [in_vmem(array) for sweep in sweeps for array in sweep]
    sums_shape = (2, samples, 2 * rank)
    sums, *totals = pl.pallas_call(
        functools.partial(fit_body, count, len(earlier)),
        compiler_params=within(16),
        grid=(1,),
        in_specs=[pl.BlockSpec(memory_space=pltpu.VMEM)] * len(arrays)
        + [pieces, pieces]
        + [whole(sums_shape)] * len(earlier),
        out_specs=[whole(sums_shape)] + [whole((rank, columns))] * count,
        out_shape=[jax.ShapeDtypeStruct(sums_shape, F32)]
        + [jax.ShapeDtypeStruct((rank, columns), F32)] * count,
        cost_estimate=cost(2 * 384 * 256 * columns * count, 32 * 64 * columns * count),
    )(*arrays, own, other, *earlier)
    return sums, totals


def eliminate(matrix, right):
    size, ahead = matrix.shape[0], 8
    whole_rows = jnp.concatenate([matrix, right], axis=1)
    groups = [whole_rows[i : i + 8] for i in range(0, size, 8)]
    lanes = whole_rows.shape[1]
    sublane = lax.broadcasted_iota(jnp.int32, (8, lanes), 0)

    def reduce(targets, columns, home, place, inverse):
        row = jnp.broadcast_to(targets[home][place : place + 1], (8, lanes)) * inverse
        reduced = [target - column * row for target, column in zip(targets, columns)]
        reduced[home] = jnp.where(sublane == place, row, reduced[home])
        return reduced

    for base in range(0, size, ahead):
        spread = [
            [jnp.broadcast_to(group[:, k : k + 1], (8, lanes)) for group in groups]
            for k in range(base, base + ahead)
        ]
        for j in range(ahead):
            home, place = divmod(base + j, 8)
            inverse = 1.0 / jnp.broadcast_to(spread[j][home][place : place + 1], (8, lanes))
            for i in range(j + 1, ahead):
                spread[i] = reduce(spread[i], spread[j], home, place, inverse)
            groups = reduce(groups, spread[j], home, place, inverse)
    return jnp.concatenate(groups, axis=0)[:, size:]


def dot32(a, b, dims=(((1,), (0,)), ((), ()))):
    return lax.dot_general(a, b, dims, precision=HIGHEST, preferred_element_type=F32)


def mix_body(*refs):
    parts, (pack_ref, scan_ref, out_ref, lcms_gram_ref) = refs[:-4], refs[-4:]
    rank = out_ref.shape[0]
    scan = scan_ref[...]
    lcms_gram = dot32(scan, scan, NT) * pack_ref[rank:, rank:]
    lcms_gram_ref[...] = lcms_gram
    gram = sum(part[...] for part in parts)
    out_ref[...] = eliminate(gram[:, :rank], lcms_gram + pack_ref[rank:, :rank])


def mix_pass(sweep, pack, scan_factor, columns):
    rank = scan_factor.shape[0]
    shape = jax.ShapeDtypeStruct((rank, rank), F32)
    return pl.pallas_call(
        mix_body,
        name="mix_pass",
        compiler_params=within(6),
        grid=(1,),
        in_specs=[pl.BlockSpec((rank, 2 * rank), lambda i: (0, columns // (2 * rank)))] * len(sweep)
        + [whole(pack.shape), whole(scan_factor.shape)],
        out_specs=[whole(shape.shape)] * 2,
        out_shape=[shape, shape],
        cost_estimate=cost(1 << 22, 65536),
    )(*sweep, pack, scan_factor)


def sample_body(*refs):
    parts, (mix_ref, lcms_gram_ref, pack_ref, out_ref) = refs[:-4], refs[-4:]
    rank = mix_ref.shape[0]
    mix = mix_ref[...]
    both = sum(part[...] for part in parts)
    fit = dot32(both[:, :rank], mix)
    new_gram = dot32(mix, dot32(both[:, rank:], mix), (((0,), (0,)), ((), ())))
    right = pack_ref[: fit.shape[0], rank:] + fit
    out_ref[...] = eliminate(lcms_gram_ref[...] + new_gram, right.T).T


def sample_pass(parts, mix, lcms_gram, pack):
    return pl.pallas_call(
        sample_body,
        name="sample_pass",
        compiler_params=within(6),
        out_shape=jax.ShapeDtypeStruct((parts[0].shape[0], mix.shape[0]), F32),
        cost_estimate=cost(1 << 22, 65536),
    )(*parts, mix, lcms_gram, pack)


def ppm_body(chip_ref, mix_ref, *refs):
    out_ref = refs[-1]
    rank = mix_ref.shape[0]
    high, low = split(mix_ref[...].T)
    left = jnp.concatenate(
        [jnp.concatenate([high, high], axis=1), jnp.concatenate([low, low], axis=1)], axis=0
    )
    start = 0
    for ref in refs[:-1]:
        products = jnp.dot(left, stack_split([ref[...]]), preferred_element_type=F32)
        out_ref[:, start : start + ref.shape[1]] = products[:rank] + products[rank:]
        start += ref.shape[1]


def ppm_pass(chip, mix, totals, direct, width):
    rank, pieces = mix.shape[0], len(totals)
    directs = [] if direct is None else [direct]
    columns = pieces * width + sum(d.shape[1] for d in directs)
    return pl.pallas_call(
        ppm_body,
        name="ppm_pass",
        compiler_params=within(12),
        grid_spec=pltpu.PrefetchScalarGridSpec(
            num_scalar_prefetch=1,
            grid=(1,),
            in_specs=[whole(mix.shape)]
            + [pl.BlockSpec((rank, width), lambda i, c: (0, c[0])) for _ in totals]
            + [whole(d.shape) for d in directs],
            out_specs=whole((rank, columns)),
        ),
        out_shape=jax.ShapeDtypeStruct((rank, columns), F32),
        cost_estimate=cost(2 * 256 * 128 * columns, 8 * 64 * columns),
    )(chip, mix, *totals, *directs)


def direct_body(chips, count, chip_ref, *refs):
    rows, refs = refs[:chips], refs[chips:]
    own, other, refs = refs[:count], refs[count : 2 * count], refs[2 * count :]
    came, swapped, projected_ref, sums_refs = refs[: chips - 1], refs[chips - 1 : 2 * chips - 2], refs[2 * chips - 2], refs[2 * chips - 1 :]
    samples, width = own[0].shape[1:]
    rank = rows[0].shape[1] // 2
    left = [wide_rows(pair[...]) for pair in rows]
    sums = [None] * chips
    gram = None
    for j in range(count):
        stacks = [stack_split([own[j][0], other[j][0]])] + [
            stack_split([came[x][j, 0], swapped[x][j, 0]]) for x in range(chips - 1)
        ]
        products = sum(
            jnp.dot(left[x], stacks[x], preferred_element_type=F32) for x in range(chips)
        )
        values = products[:rank] + products[rank:]
        projected_ref[:, j * width : (j + 1) * width] = values
        right = stack_split([values])
        for x in range(chips):
            fit = lax.dot_general(stacks[x], right, NT, preferred_element_type=F32)
            sums[x] = fit if j == 0 else sums[x] + fit
        square = lax.dot_general(right, right, NT, preferred_element_type=F32)
        gram = square if j == 0 else gram + square
    gram = gram[:rank] + gram[rank:]
    gram = gram[:, :rank] + gram[:, rank:]
    for x in range(chips):
        fit = sums[x][: 2 * samples] + sums[x][2 * samples :]
        fit = fit[:, :rank] + fit[:, rank:]
        for side in (0, 1):
            sums_refs[x][side] = jnp.concatenate([fit[side * samples : (side + 1) * samples], gram], axis=1)


def direct_pass(chip, rows, own, other, came, swapped, first):
    chips, count = len(rows), own.shape[0] - first
    samples, rank = own.shape[1], rows[0].shape[1] // 2
    width = came[0].shape[3]
    pieces = [
        pl.BlockSpec((1, samples, width), functools.partial(lambda j, i, c: (first + j, 0, c[0]), j))
        for j in range(count)
    ]
    return pl.pallas_call(
        functools.partial(direct_body, chips, count),
        name="direct_pass",
        compiler_params=within(16),
        grid_spec=pltpu.PrefetchScalarGridSpec(
            num_scalar_prefetch=1,
            grid=(1,),
            in_specs=[whole(r.shape) for r in rows]
            + pieces
            + pieces
            + [pl.BlockSpec((count, 1, samples, width), lambda i, c: (0, 0, 0, 0))] * (chips - 1)
            + [pl.BlockSpec((count, 1, samples, width), lambda i, c: (0, 1, 0, 0))] * (chips - 1),
            out_specs=[whole((rank, count * width))] + [whole((2, samples, 2 * rank))] * chips,
        ),
        out_shape=[jax.ShapeDtypeStruct((rank, count * width), F32)]
        + [jax.ShapeDtypeStruct((2, samples, 2 * rank), F32)] * chips,
        cost_estimate=cost(2 * 512 * 512 * count * width * 2, 4 * 512 * count * width),
    )(chip, *rows, *([own] * count), *([other] * count), *came, *swapped)


def from_mz(values, count):
    result = [values]
    for step in range(1, count):
        hops = [(i, (i + step) % count) for i in range(count)]
        result.append(lax.ppermute(values, "mz", hops))
    return result


def from_chips(values, runs):
    chips = runs // 2
    return [
        lax.ppermute(values[step - 1], "run", [(i, i ^ (2 * step)) for i in range(runs)])
        for step in range(1, chips)
    ]


def sum_over_chips(parts, runs):
    lines = [4 * line for line in range(runs // 8)]

    def send(values, pairs):
        hops = [
            (2 * (line + a) + core, 2 * (line + b) + core) for line in lines for a, b in pairs for core in (0, 1)
        ]
        return lax.ppermute(values, "run", hops)

    sweeps = []
    for part in parts:
        inward = send(part, [(0, 1), (3, 2)])
        across = send(part + inward, [(1, 2), (2, 1)])
        outward = send(part + across, [(1, 0), (2, 3)])
        if len(lines) > 1:
            line_total = part + inward + across + outward
            for step in range(1, len(lines)):
                shifted = [(i, (i + 8 * step) % runs) for i in range(runs)]
                part = part + lax.ppermute(line_total, "run", shifted)
        sweeps.append((part, inward, across, outward))
    return sweeps


def per_device(runs, mzs, lcms, spectra, scan_factor, mz_factor, ppm_factor):
    _, positions = spectra.shape
    chips = runs // 2
    width = positions // runs
    pieces = min(8, width // 128)
    swept = pieces // 2 if chips == 4 else pieces
    width = width // pieces
    run = lax.axis_index("run").astype(jnp.int32)
    core, chip = (run % 2).reshape(1), (run // 2).reshape(1)
    swap = [(i, i ^ 1) for i in range(runs)]

    spectra = pltpu.with_memory_space_constraint(spectra, pltpu.HBM)
    own, leaving, *parcels = sort_pass(core, chip, spectra, chips, pieces, swept)
    came = from_chips(parcels, runs) if parcels else []
    other = lax.ppermute(leaving, "run", swap)
    part = nmr_pass(core, own, leaving, ppm_factor, mz_factor, chips)
    pack = lcms_pass(lcms, scan_factor, mz_factor, part)
    pack = sum(from_mz(pack, mzs))
    left, rows, first = first_pass(pack, lax.ppermute(pack, "run", swap), own, other)
    sweeps = sum_over_chips([first, *project_pass(left, own, other, 1, swept - 1)], runs)
    projected, direct = None, []
    if parcels:
        rows = [rows] + from_chips([rows] * (chips - 1), runs)
        swapped = [lax.ppermute(array, "run", swap) for array in came]
        projected, *sums = direct_pass(chip, rows, own, other, came, swapped, swept)
        direct = sums[:1] + from_chips(sums[1:], runs)
    totals, sums = [], []
    for k in range(0, swept, 2):
        earlier = sums + (direct if k + 2 == swept else [])
        sums, done = fit_pass(sweeps[k : k + 2], earlier, own, other, k)
        totals, sums = totals + done, [sums]
    mix, lcms_gram = mix_pass(sweeps[0], pack, scan_factor, own.shape[2])
    ppm_new = ppm_pass(chip, mix, totals, projected, width)
    fits = from_mz(sums[0][0] + lax.ppermute(sums[0], "run", swap)[1], mzs)
    sample_factor = sample_pass(fits, mix, lcms_gram, pack)
    return (sample_factor, ppm_new)


def solution(mesh):
    runs, mzs = mesh.shape["run"], mesh.shape["mz"]

    def whole_step(lcms, spectra, scan_factor, mz_factor, ppm_factor):
        return per_device(runs, mzs, lcms, spectra, scan_factor, mz_factor, ppm_factor)

    return jax.shard_map(
        whole_step,
        mesh=mesh,
        in_specs=(P("run", None, "mz"), P("run", "mz"), P(), P(None, "mz"), P(None, "mz")),
        out_specs=(P("run", None), P(None, ("mz", "run"))),
        check_vma=False,
    )
```

```python
import functools

import jax
import jax.numpy as jnp
from jax import lax
from jax.experimental import pallas as pl
from jax.experimental.pallas import tpu as pltpu
from jax.sharding import PartitionSpec as P


F32, BF16 = jnp.float32, jnp.bfloat16
HIGHEST = lax.Precision.HIGHEST
NT = (((1,), (1,)), ((), ()))


def split(values):
    high = values.astype(BF16)
    return high, (values - high.astype(F32)).astype(BF16)


def stack_split(blocks):
    pairs = [split(block) for block in blocks]
    return jnp.concatenate([pair[0] for pair in pairs] + [pair[1] for pair in pairs], axis=0)


def cost(flops, transferred):
    return pl.CostEstimate(flops=int(flops), bytes_accessed=int(transferred), transcendentals=0)


def within(mebibytes):
    return pltpu.CompilerParams(vmem_limit_bytes=mebibytes << 20)


def in_vmem(array):
    return pltpu.with_memory_space_constraint(array, pltpu.VMEM)


def whole(shape):
    return pl.BlockSpec(shape, lambda *_: (0,) * len(shape))


def sort_body(blocks, first, core_ref, chip_ref, *refs):
    spectra_refs, (keep_ref, send_ref, *parcels) = refs[: 2 * blocks], refs[2 * blocks :]
    count, width = keep_ref.shape[0], keep_ref.shape[2] // blocks
    for core in (0, 1):

        @pl.when(core_ref[0] == core)
        def _():
            for b in range(blocks):
                for j in range(count):
                    taken = slice(j * width, (j + 1) * width)
                    keep_ref[j, :, b * width : (b + 1) * width] = spectra_refs[2 * b + core][:, taken]
                    send_ref[j, :, b * width : (b + 1) * width] = spectra_refs[2 * b + 1 - core][:, taken]

    if parcels:

        @pl.when(pl.program_id(0) >= first)
        def _():
            for step, parcel in enumerate(parcels, 1):
                columns = pl.ds(pl.multiple_of((chip_ref[0] ^ step) * width, width), width)
                for j in range(count):
                    parcel[j, 0] = keep_ref[j, :, columns]
                    parcel[j, 1] = send_ref[j, :, columns]


def sort_pass(core, chip, spectra, blocks, pieces, swept):
    samples, positions = spectra.shape
    width = positions // (2 * blocks * pieces)
    count = 2 if pieces % 2 == 0 and swept % 2 == 0 else 1
    steps, first = pieces // count, swept // count
    columns = [
        pl.BlockSpec((samples, count * width), functools.partial(lambda b, k, c, h: (0, b * steps + k), b))
        for b in range(2 * blocks)
    ]
    sorted_shape = jax.ShapeDtypeStruct((pieces, samples, blocks * width), F32)
    parcels = blocks - 1 if swept < pieces else 0
    parcel_shape = jax.ShapeDtypeStruct((pieces - swept, 2, samples, width), F32)
    parcel_spec = pl.BlockSpec((count, 2, samples, width), lambda k, c, h: (jnp.maximum(k - first, 0), 0, 0, 0))
    return pl.pallas_call(
        functools.partial(sort_body, blocks, first),
        name="sort_pass",
        compiler_params=within(16),
        grid_spec=pltpu.PrefetchScalarGridSpec(
            num_scalar_prefetch=2,
            grid=(steps,),
            in_specs=columns,
            out_specs=[pl.BlockSpec((count, samples, blocks * width), lambda k, c, h: (k, 0, 0))] * 2
            + [parcel_spec] * parcels,
        ),
        out_shape=[sorted_shape, sorted_shape] + [parcel_shape] * parcels,
        cost_estimate=cost(1 << 20, 4 * 2 * 64 * positions),
    )(core, chip, *([spectra] * (2 * blocks)))


def nmr_body(blocks, core_ref, keep_ref, send_ref, *refs):
    ppm_refs, (mz_ref, part_ref, total) = refs[: 2 * blocks], refs[2 * blocks :]
    piece = pl.program_id(0)
    rank = mz_ref.shape[0]

    @pl.when(piece == 0)
    def _():
        total[...] = jnp.zeros_like(total)
        channels = stack_split([mz_ref[...]])
        products = lax.dot_general(channels, channels, NT, preferred_element_type=F32)
        rows = products[:rank] + products[rank:]
        part_ref[:, rank:] = jnp.zeros_like(part_ref[:, rank:])
        part_ref[rank:, rank:] = rows[:, :rank] + rows[:, rank:]

    values = jnp.concatenate([keep_ref[0], send_ref[0]], axis=1)
    positions = stack_split([jnp.concatenate([ref[...] for ref in ppm_refs], axis=1)])
    left = jnp.concatenate([stack_split([values]), positions[:rank]], axis=0)
    total[...] += lax.dot_general(left, positions, NT, preferred_element_type=F32)

    @pl.when(piece == pl.num_programs(0) - 1)
    def _():
        samples = keep_ref.shape[1]
        products = total[...]
        fit = products[:samples] + products[samples : 2 * samples]
        gram = products[2 * samples :]
        mixed = gram[:, rank:]
        part_ref[:rank, :rank] = fit[:, :rank] + fit[:, rank:]
        part_ref[rank:, :rank] = gram[:, :rank] + (mixed + mixed.T)


def nmr_pass(core, keep, send, ppm_factor, mz_factor, blocks):
    pieces, samples, columns = keep.shape
    rank, channels = mz_factor.shape
    width = columns // blocks

    def positions(side):
        return [
            pl.BlockSpec(
                (rank, width),
                functools.partial(lambda b, k, c: (0, (2 * b + (c[0] ^ side)) * pieces + k), b),
            )
            for b in range(blocks)
        ]

    piece = pl.BlockSpec((1, samples, columns), lambda k, c: (k, 0, 0))
    return pl.pallas_call(
        functools.partial(nmr_body, blocks),
        name="nmr_pass",
        compiler_params=within(16),
        grid_spec=pltpu.PrefetchScalarGridSpec(
            num_scalar_prefetch=1,
            grid=(pieces,),
            in_specs=[piece, piece] + positions(0) + positions(1) + [whole((rank, channels))],
            out_specs=whole((2 * rank, 2 * rank)),
            scratch_shapes=[pltpu.VMEM((2 * samples + rank, 2 * rank), F32)],
        ),
        out_shape=jax.ShapeDtypeStruct((2 * rank, 2 * rank), F32),
        cost_estimate=cost(2 * 256 * 256 * pieces * columns, 4 * 3 * 64 * pieces * columns),
    )(core, keep, send, *([ppm_factor] * (2 * blocks)), mz_factor)


def lcms_body(lcms_ref, scan_ref, mz_ref, part_ref, out_ref, weights, scans):
    rank = mz_ref.shape[0]
    step = pl.program_id(0)
    count, steps, channels = lcms_ref.shape

    @pl.when(step == 0)
    def _():
        high, low = split(mz_ref[...].T)
        weights[...] = jnp.concatenate([high, low], axis=1)
        scan = scan_ref[...].astype(BF16).astype(F32).T
        scans[...] = jnp.concatenate([scan, scan], axis=1)
        out_ref[rank:, :] = part_ref[rank:, :]

    inner = jnp.dot(
        lcms_ref[...].reshape(count * steps, channels), weights[...], preferred_element_type=F32
    )
    sums = jnp.sum(inner.reshape(count, steps, 2 * rank) * scans[...][None], axis=1)
    rows = pl.ds(pl.multiple_of(step * count, count), count)
    out_ref[rows, :] = sums + pltpu.roll(sums, rank, 1) + part_ref[rows, :]


def lcms_pass(lcms, scan_factor, mz_factor, part):
    samples, steps, channels = lcms.shape
    rank = mz_factor.shape[0]
    count = 16
    return pl.pallas_call(
        lcms_body,
        name="lcms_pass",
        compiler_params=within(32),
        grid=(samples // count,),
        in_specs=[
            pl.BlockSpec((count, steps, channels), lambda i: (i, 0, 0)),
            whole(scan_factor.shape),
            whole(mz_factor.shape),
            whole(part.shape),
        ],
        out_specs=whole(part.shape),
        out_shape=jax.ShapeDtypeStruct(part.shape, F32),
        scratch_shapes=[
            pltpu.VMEM((channels, 2 * rank), BF16),
            pltpu.VMEM((steps, 2 * rank), F32),
        ],
        cost_estimate=cost(2 * samples * steps * channels * 256, 2 * samples * steps * channels),
    )(lcms, scan_factor, mz_factor, part)


def first_body(own_pack, other_pack, own_ref, other_ref, left_ref, rows_ref, out_ref):
    rank, columns = rows_ref.shape[1] // 2, own_ref.shape[2]
    samples = own_ref.shape[1]
    rows = jnp.concatenate([own_pack[:samples, :rank], other_pack[:samples, :rank]], axis=1)
    rows_ref[...] = rows
    left = wide_rows(rows)
    left_ref[...] = left
    sides = [(own_ref[0], other_ref[0], 0), (rows[:, :rank], rows[:, rank:], columns)]
    for own, other, start in sides:
        products = jnp.dot(left, stack_split([own, other]), preferred_element_type=F32)
        out_ref[:, start : start + own.shape[1]] = products[:rank] + products[rank:]
    out_ref[:, columns + rank :] = jnp.zeros_like(out_ref[:, columns + rank :])


def wide_rows(rows):
    rank = rows.shape[1] // 2
    turned = rows.T
    return jnp.concatenate(
        [
            jnp.concatenate([part[:rank], part[rank:], part[:rank], part[rank:]], axis=1)
            for part in split(turned)
        ],
        axis=0,
    )


def first_pass(own_pack, other_pack, own, other):
    _, samples, columns = own.shape
    rank = own_pack.shape[1] // 2
    piece = pl.BlockSpec((1, samples, columns), lambda k: (0, 0, 0))
    return pl.pallas_call(
        first_body,
        name="first_pass",
        compiler_params=within(12),
        grid=(1,),
        in_specs=[whole(own_pack.shape)] * 2 + [piece] * 2,
        out_specs=[
            whole((2 * rank, 4 * samples)),
            whole((samples, 2 * rank)),
            whole((rank, columns + 2 * rank)),
        ],
        out_shape=[
            jax.ShapeDtypeStruct((2 * rank, 4 * samples), BF16),
            jax.ShapeDtypeStruct((samples, 2 * rank), F32),
            pltpu.VMEM((rank, columns + 2 * rank), F32),
        ],
        cost_estimate=cost(2 * 256 * 256 * columns, 12 * 64 * columns),
    )(own_pack, other_pack, own, other)


def project_body(left_ref, own_ref, other_ref, *outs):
    rank = left_ref.shape[0] // 2
    right = stack_split([own_ref[0], other_ref[0]])
    products = jnp.dot(left_ref[...], right, preferred_element_type=F32)
    values = products[:rank] + products[rank:]
    for k, out_ref in enumerate(outs):

        @pl.when(pl.program_id(0) == k)
        def _():
            out_ref[...] = values


def project_pass(left, own, other, first, count):
    _, samples, columns = own.shape
    rank = left.shape[0] // 2
    piece = pl.BlockSpec((1, samples, columns), lambda k: (first + k, 0, 0))
    return pl.pallas_call(
        project_body,
        name="project_pass",
        compiler_params=within(12),
        grid=(count,),
        in_specs=[whole(left.shape), piece, piece],
        out_specs=[whole((rank, columns))] * count,
        out_shape=[pltpu.VMEM((rank, columns), F32)] * count,
        cost_estimate=cost(2 * 256 * 256 * columns * count, 12 * 64 * columns * count),
    )(left, own, other)


def fit_body(count, earlier, *refs):
    sweeps, refs = refs[: 4 * count], refs[4 * count :]
    own_ref, other_ref, sums_ref = refs[0], refs[1], refs[2 + earlier]
    _, samples, columns = own_ref.shape
    rank = sums_ref.shape[2] // 2
    sums = None
    for k in range(count):
        part, inward, across, outward = (ref[:, :columns] for ref in sweeps[4 * k : 4 * k + 4])
        total = part + inward + across + outward
        refs[3 + earlier + k][...] = total
        right = stack_split([total])
        rows = jnp.concatenate([stack_split([own_ref[k], other_ref[k]]), right], axis=0)
        products = lax.dot_general(rows, right, NT, preferred_element_type=F32)
        sums = products if sums is None else sums + products
    sums = sums[:, :rank] + sums[:, rank:]
    gram = sums[4 * samples : 4 * samples + rank] + sums[4 * samples + rank :]
    fits = [
        sums[side * samples : (side + 1) * samples] + sums[(side + 2) * samples : (side + 3) * samples]
        for side in (0, 1)
    ]
    for ref in refs[2 : 2 + earlier]:
        if len(ref.shape) == 3:
            continue
        fits = [fits[side] + ref[:samples, side * rank : (side + 1) * rank] for side in (0, 1)]
        gram = gram + jnp.concatenate([ref[samples:, :rank], ref[samples:, rank:]], axis=0)
    for side in (0, 1):
        total = jnp.concatenate([fits[side], gram], axis=1)
        for ref in refs[2 : 2 + earlier]:
            if len(ref.shape) == 3:
                total = total + ref[side]
        sums_ref[side] = total


def fit_pass(sweeps, earlier, own, other, first):
    _, samples, columns = own.shape
    count, rank = len(sweeps), sweeps[0][0].shape[0]
    pieces = pl.BlockSpec((count, samples, columns), lambda i: (first // count, 0, 0))
    assert first % count == 0
    arrays = [in_vmem(array) for sweep in sweeps for array in sweep]
    sums_shape = (2, samples, 2 * rank)
    sums, *totals = pl.pallas_call(
        functools.partial(fit_body, count, len(earlier)),
        compiler_params=within(16),
        grid=(1,),
        in_specs=[pl.BlockSpec(memory_space=pltpu.VMEM)] * len(arrays)
        + [pieces, pieces]
        + [whole(array.shape) for array in earlier],
        out_specs=[whole(sums_shape)] + [whole((rank, columns))] * count,
        out_shape=[jax.ShapeDtypeStruct(sums_shape, F32)]
        + [jax.ShapeDtypeStruct((rank, columns), F32)] * count,
        cost_estimate=cost(2 * 384 * 256 * columns * count, 32 * 64 * columns * count),
    )(*arrays, own, other, *earlier)
    return sums, totals


def eliminate(matrix, right):
    size, ahead = matrix.shape[0], 8
    whole_rows = jnp.concatenate([matrix, right], axis=1)
    groups = [whole_rows[i : i + 8] for i in range(0, size, 8)]
    lanes = whole_rows.shape[1]
    sublane = lax.broadcasted_iota(jnp.int32, (8, lanes), 0)

    def reduce(targets, columns, home, place, inverse):
        row = jnp.broadcast_to(targets[home][place : place + 1], (8, lanes)) * inverse
        reduced = [target - column * row for target, column in zip(targets, columns)]
        reduced[home] = jnp.where(sublane == place, row, reduced[home])
        return reduced

    for base in range(0, size, ahead):
        spread = [
            [jnp.broadcast_to(group[:, k : k + 1], (8, lanes)) for group in groups]
            for k in range(base, base + ahead)
        ]
        for j in range(ahead):
            home, place = divmod(base + j, 8)
            inverse = 1.0 / jnp.broadcast_to(spread[j][home][place : place + 1], (8, lanes))
            for i in range(j + 1, ahead):
                spread[i] = reduce(spread[i], spread[j], home, place, inverse)
            groups = reduce(groups, spread[j], home, place, inverse)
    return jnp.concatenate(groups, axis=0)[:, size:]


def dot32(a, b, dims=(((1,), (0,)), ((), ()))):
    return lax.dot_general(a, b, dims, precision=HIGHEST, preferred_element_type=F32)


def mix_body(*refs):
    parts, (pack_ref, scan_ref, out_ref, lcms_gram_ref) = refs[:-4], refs[-4:]
    rank = out_ref.shape[0]
    scan = scan_ref[...]
    lcms_gram = dot32(scan, scan, NT) * pack_ref[rank:, rank:]
    lcms_gram_ref[...] = lcms_gram
    gram = sum(part[...] for part in parts)
    out_ref[...] = eliminate(gram[:, :rank], lcms_gram + pack_ref[rank:, :rank])


def mix_pass(sweep, pack, scan_factor, columns):
    rank = scan_factor.shape[0]
    shape = jax.ShapeDtypeStruct((rank, rank), F32)
    return pl.pallas_call(
        mix_body,
        name="mix_pass",
        compiler_params=within(6),
        grid=(1,),
        in_specs=[pl.BlockSpec((rank, 2 * rank), lambda i: (0, columns // (2 * rank)))] * len(sweep)
        + [whole(pack.shape), whole(scan_factor.shape)],
        out_specs=[whole(shape.shape)] * 2,
        out_shape=[shape, shape],
        cost_estimate=cost(1 << 22, 65536),
    )(*sweep, pack, scan_factor)


def sample_body(*refs):
    parts, (mix_ref, lcms_gram_ref, pack_ref, out_ref) = refs[:-4], refs[-4:]
    rank = mix_ref.shape[0]
    mix = mix_ref[...]
    both = sum(part[...] for part in parts)
    fit = dot32(both[:, :rank], mix)
    new_gram = dot32(mix, dot32(both[:, rank:], mix), (((0,), (0,)), ((), ())))
    right = pack_ref[: fit.shape[0], rank:] + fit
    out_ref[...] = eliminate(lcms_gram_ref[...] + new_gram, right.T).T


def sample_pass(parts, mix, lcms_gram, pack):
    return pl.pallas_call(
        sample_body,
        name="sample_pass",
        compiler_params=within(6),
        out_shape=jax.ShapeDtypeStruct((parts[0].shape[0], mix.shape[0]), F32),
        cost_estimate=cost(1 << 22, 65536),
    )(*parts, mix, lcms_gram, pack)


def ppm_body(chip_ref, mix_ref, *refs):
    out_ref = refs[-1]
    rank = mix_ref.shape[0]
    high, low = split(mix_ref[...].T)
    left = jnp.concatenate(
        [jnp.concatenate([high, high], axis=1), jnp.concatenate([low, low], axis=1)], axis=0
    )
    start = 0
    for ref in refs[:-1]:
        products = jnp.dot(left, stack_split([ref[...]]), preferred_element_type=F32)
        out_ref[:, start : start + ref.shape[1]] = products[:rank] + products[rank:]
        start += ref.shape[1]


def ppm_pass(chip, mix, totals, direct, width):
    rank, pieces = mix.shape[0], len(totals)
    directs = [] if direct is None else [direct]
    columns = pieces * width + sum(d.shape[1] for d in directs)
    return pl.pallas_call(
        ppm_body,
        name="ppm_pass",
        compiler_params=within(12),
        grid_spec=pltpu.PrefetchScalarGridSpec(
            num_scalar_prefetch=1,
            grid=(1,),
            in_specs=[whole(mix.shape)]
            + [pl.BlockSpec((rank, width), lambda i, c: (0, c[0])) for _ in totals]
            + [whole(d.shape) for d in directs],
            out_specs=whole((rank, columns)),
        ),
        out_shape=jax.ShapeDtypeStruct((rank, columns), F32),
        cost_estimate=cost(2 * 256 * 128 * columns, 8 * 64 * columns),
    )(chip, mix, *totals, *directs)


def direct_body(chips, count, chip_ref, *refs):
    rows, refs = refs[:chips], refs[chips:]
    own, other, refs = refs[:count], refs[count : 2 * count], refs[2 * count :]
    came, swapped, projected_ref, sums_refs = refs[: chips - 1], refs[chips - 1 : 2 * chips - 2], refs[2 * chips - 2], refs[2 * chips - 1 :]
    samples, width = own[0].shape[1:]
    rank = rows[0].shape[1] // 2
    left = [wide_rows(pair[...]) for pair in rows]
    sums = [None] * chips
    gram = None
    for j in range(count):
        stacks = [stack_split([own[j][0], other[j][0]])] + [
            stack_split([came[x][j, 0], swapped[x][j, 0]]) for x in range(chips - 1)
        ]
        products = sum(
            jnp.dot(left[x], stacks[x], preferred_element_type=F32) for x in range(chips)
        )
        values = products[:rank] + products[rank:]
        projected_ref[:, j * width : (j + 1) * width] = values
        right = stack_split([values])
        for x in range(chips):
            fit = lax.dot_general(stacks[x], right, NT, preferred_element_type=F32)
            sums[x] = fit if j == 0 else sums[x] + fit
        square = lax.dot_general(right, right, NT, preferred_element_type=F32)
        gram = square if j == 0 else gram + square
    gram = gram[:rank] + gram[rank:]
    gram = gram[:, :rank] + gram[:, rank:]
    for x in range(chips):
        fit = sums[x][: 2 * samples] + sums[x][2 * samples :]
        fit = fit[:, :rank] + fit[:, rank:]
        sums_refs[x][:samples] = jnp.concatenate([fit[:samples], fit[samples:]], axis=1)
        sums_refs[x][samples:] = jnp.concatenate([gram[: rank // 2], gram[rank // 2 :]], axis=1)


def direct_pass(chip, rows, own, other, came, swapped, first):
    chips, count = len(rows), own.shape[0] - first
    samples, rank = own.shape[1], rows[0].shape[1] // 2
    width = came[0].shape[3]
    pieces = [
        pl.BlockSpec((1, samples, width), functools.partial(lambda j, i, c: (first + j, 0, c[0]), j))
        for j in range(count)
    ]
    return pl.pallas_call(
        functools.partial(direct_body, chips, count),
        name="direct_pass",
        compiler_params=within(16),
        grid_spec=pltpu.PrefetchScalarGridSpec(
            num_scalar_prefetch=1,
            grid=(1,),
            in_specs=[whole(r.shape) for r in rows]
            + pieces
            + pieces
            + [pl.BlockSpec((count, 1, samples, width), lambda i, c: (0, 0, 0, 0))] * (chips - 1)
            + [pl.BlockSpec((count, 1, samples, width), lambda i, c: (0, 1, 0, 0))] * (chips - 1),
            out_specs=[whole((rank, count * width))] + [whole((samples + rank // 2, 2 * rank))] * chips,
        ),
        out_shape=[jax.ShapeDtypeStruct((rank, count * width), F32)]
        + [jax.ShapeDtypeStruct((samples + rank // 2, 2 * rank), F32)] * chips,
        cost_estimate=cost(2 * 512 * 512 * count * width * 2, 4 * 512 * count * width),
    )(chip, *rows, *([own] * count), *([other] * count), *came, *swapped)


def from_mz(values, count):
    result = [values]
    for step in range(1, count):
        hops = [(i, (i + step) % count) for i in range(count)]
        result.append(lax.ppermute(values, "mz", hops))
    return result


def from_chips(values, runs):
    chips = runs // 2
    return [
        lax.ppermute(values[step - 1], "run", [(i, i ^ (2 * step)) for i in range(runs)])
        for step in range(1, chips)
    ]


def sum_over_chips(parts, runs):
    lines = [4 * line for line in range(runs // 8)]

    def send(values, pairs):
        hops = [
            (2 * (line + a) + core, 2 * (line + b) + core) for line in lines for a, b in pairs for core in (0, 1)
        ]
        return lax.ppermute(values, "run", hops)

    sweeps = []
    for part in parts:
        inward = send(part, [(0, 1), (3, 2)])
        across = send(part + inward, [(1, 2), (2, 1)])
        outward = send(part + across, [(1, 0), (2, 3)])
        if len(lines) > 1:
            line_total = part + inward + across + outward
            for step in range(1, len(lines)):
                shifted = [(i, (i + 8 * step) % runs) for i in range(runs)]
                part = part + lax.ppermute(line_total, "run", shifted)
        sweeps.append((part, inward, across, outward))
    return sweeps


def per_device(runs, mzs, lcms, spectra, scan_factor, mz_factor, ppm_factor):
    _, positions = spectra.shape
    chips = runs // 2
    width = positions // runs
    pieces = min(8, width // 128)
    swept = pieces // 2 if chips == 4 else pieces
    width = width // pieces
    run = lax.axis_index("run").astype(jnp.int32)
    core, chip = (run % 2).reshape(1), (run // 2).reshape(1)
    swap = [(i, i ^ 1) for i in range(runs)]

    spectra = pltpu.with_memory_space_constraint(spectra, pltpu.HBM)
    own, leaving, *parcels = sort_pass(core, chip, spectra, chips, pieces, swept)
    came = from_chips(parcels, runs) if parcels else []
    other = lax.ppermute(leaving, "run", swap)
    part = nmr_pass(core, own, leaving, ppm_factor, mz_factor, chips)
    pack = lcms_pass(lcms, scan_factor, mz_factor, part)
    pack = sum(from_mz(pack, mzs))
    left, rows, first = first_pass(pack, lax.ppermute(pack, "run", swap), own, other)
    sweeps = sum_over_chips([first, *project_pass(left, own, other, 1, swept - 1)], runs)
    projected, direct = None, []
    if parcels:
        rows = [rows] + from_chips([rows] * (chips - 1), runs)
        swapped = [lax.ppermute(array, "run", swap) for array in came]
        projected, *sums = direct_pass(chip, rows, own, other, came, swapped, swept)
        direct = sums[:1] + from_chips(sums[1:], runs)
    totals, sums = [], []
    for k in range(0, swept, 2):
        earlier = sums + (direct if k + 2 == swept else [])
        sums, done = fit_pass(sweeps[k : k + 2], earlier, own, other, k)
        totals, sums = totals + done, [sums]
    mix, lcms_gram = mix_pass(sweeps[0], pack, scan_factor, own.shape[2])
    ppm_new = ppm_pass(chip, mix, totals, projected, width)
    fits = from_mz(sums[0][0] + lax.ppermute(sums[0], "run", swap)[1], mzs)
    sample_factor = sample_pass(fits, mix, lcms_gram, pack)
    return (sample_factor, ppm_new)


def solution(mesh):
    runs, mzs = mesh.shape["run"], mesh.shape["mz"]

    def whole_step(lcms, spectra, scan_factor, mz_factor, ppm_factor):
        return per_device(runs, mzs, lcms, spectra, scan_factor, mz_factor, ppm_factor)

    return jax.shard_map(
        whole_step,
        mesh=mesh,
        in_specs=(P("run", None, "mz"), P("run", "mz"), P(), P(None, "mz"), P(None, "mz")),
        out_specs=(P("run", None), P(None, ("mz", "run"))),
        check_vma=False,
    )
```
